256 devices in a mesh: grp: 8 (over y, x_hi), tp: 32 (over z, x_lo, core).
Axes of the slice: x: 4 (x_hi: 2, x_lo: 2; x = x_hi * 2 + x_lo), y: 4, z: 8, core: 2. Of those that a mesh axis runs over, the one named last changes fastest.
Arguments:
- key_cache: bfloat16 [8, 32, 768, 512], P('grp', 'tp'), may hold values from -6 to 6
- value_cache: bfloat16 [8, 32, 768, 512], P('grp', 'tp'), may hold values from -12 to 12
- lengths: int32 [8, 32], P('grp', 'tp'), may hold values from 256 to 768, as said below
- queries: bfloat16 [8, 1, 32, 8192], P('grp', None, 'tp'), may hold values from -12 to 12
- new_keys: bfloat16 [8, 1, 32, 512], P('grp', None, 'tp'), may hold values from -18 to 18
- new_values: bfloat16 [8, 1, 32, 512], P('grp', None, 'tp'), may hold values from -12 to 12
- residual: bfloat16 [8, 1, 32, 8192], P('grp', None, 'tp'), may hold values from -4 to 4
- norm_gain: float32 [8192], replicated, may hold values from 0.25 to 1.75
- gate_weight: bfloat16 [8, 6656, 8192], P('grp', 'tp'), may hold values from -0.0625 to 0.0625
- up_weight: bfloat16 [8, 6656, 8192], P('grp', 'tp'), may hold values from -0.0625 to 0.0625
- down_weight: bfloat16 [8, 6656, 8192], P('grp', 'tp'), may hold values from -0.0390625 to 0.0390625
Outputs:
- mixed: bfloat16 [8, 1, 32, 8192], P('grp', None, 'tp')
The draws below stay inside these ranges and needn't reach their ends.
Inputs may be any that keep to these rules, and one draw needn't show every extreme that they name: `lengths`: some row has exactly 768 valid positions.
All inputs are finite; a program needn't handle non-finite values.
Results may differ from the reference program's by a relative error of at most 0.005.
Values may be sent and summed in bfloat16 or wider, within the bound.
No kernel may reach another device: no remote copies, remote signals or barrier semaphores. Data moves between devices by JAX's collectives and lax.ppermute only.
A program may use at most 64 MiB of HBM per device.

```python
import jax
import jax.numpy as jnp
from jax import lax

D = 8192
HEADS = 64
HD = 128
KVH = 4
FF = 26624
CAP = 768
STEPS = 1
AGROUPS = 4
GROUP_ROWS = 32
N_GRP = 8


def draw_key_cache(key, part):
    shape = (N_GRP, GROUP_ROWS, CAP, KVH * HD)
    base = jax.random.truncated_normal(jax.random.fold_in(key, 11), -6.0, 6.0, shape)
    return base.astype(jnp.bfloat16)


def draw_queries(key, part):
    shape = (N_GRP, STEPS, GROUP_ROWS, D)
    base = 2.5 * jax.random.truncated_normal(jax.random.fold_in(key, 12), -4.8, 4.8, shape)
    return base.astype(jnp.bfloat16)


def draw_lengths(key, part):
    reach = CAP // 3
    spread = jax.random.randint(jax.random.fold_in(key, 21), (N_GRP, GROUP_ROWS), 0, CAP - reach + 1)
    group = jnp.arange(N_GRP) % (N_GRP // 2)
    length = reach + spread * (group[:, None] + 1) // (N_GRP // 2)
    peak_row = jax.random.randint(jax.random.fold_in(key, 22), (), 0, GROUP_ROWS)
    mark = (jnp.arange(N_GRP)[:, None] == N_GRP // 2 - 1) & (jnp.arange(GROUP_ROWS)[None, :] == peak_row)
    return jnp.where(mark, CAP, length).astype(jnp.int32)


def draw_residual(key, part):
    shape = (N_GRP, STEPS, GROUP_ROWS, D)
    base = jax.random.truncated_normal(jax.random.fold_in(key, 31), -6.0, 6.0, shape)
    return (0.5 * base).astype(jnp.bfloat16)


def levels(own_key, extent, cuts, low, high):
    factor_of = 1.0
    for dim, shards_of in cuts:
        draws = jax.random.uniform(jax.random.fold_in(jax.random.fold_in(own_key, 6), dim), (shards_of,), jnp.float32, low / len(cuts), high / len(cuts))
        factor_of = factor_of * jnp.repeat(jnp.exp(draws), extent[dim] // shards_of).reshape((-1,) + (1,) * (len(extent) - 1 - dim))
    return factor_of


def scatter_about(key, dims, scale, limit, shards=(), held_as=jnp.bfloat16):
    loudness = levels(key, dims, shards, -0.22, 0.18) if shards else 1.0
    values = jax.random.normal(key, dims, jnp.float32) * scale * loudness
    return jnp.minimum(jnp.maximum(values, -limit), limit).astype(held_as)


def setup_inputs(seed: int = 0) -> dict:
    splits = jax.random.split(jax.random.key(seed), 12)
    return {
        "key_cache": draw_key_cache(jax.random.fold_in(splits[11], 71), 0),
        "value_cache": scatter_about(splits[1], (N_GRP, GROUP_ROWS, CAP, KVH * HD), 2.0, 12.0, ((0, 8), (1, 32))),
        "lengths": draw_lengths(jax.random.fold_in(splits[11], 71), 0),
        "queries": draw_queries(jax.random.fold_in(splits[11], 71), 0),
        "new_keys": scatter_about(splits[4], (N_GRP, STEPS, GROUP_ROWS, KVH * HD), 3.0, 18.0, ((0, 8), (2, 32))),
        "new_values": scatter_about(splits[5], (N_GRP, STEPS, GROUP_ROWS, KVH * HD), 2.0, 12.0, ((0, 8), (2, 32))),
        "residual": draw_residual(jax.random.fold_in(splits[11], 71), 0),
        "norm_gain": jnp.clip(1.0 + 0.15 * jax.random.normal(splits[7], (D,), jnp.float32), 0.25, 1.75),
        "gate_weight": scatter_about(splits[8], (N_GRP, FF // AGROUPS, D), D ** -0.5, 0.0625, ((0, 8), (1, 32))),
        "up_weight": scatter_about(splits[9], (N_GRP, FF // AGROUPS, D), D ** -0.5, 0.0625, ((0, 8), (1, 32))),
        "down_weight": scatter_about(splits[10], (N_GRP, FF // AGROUPS, D), FF ** -0.5, 0.0390625, ((0, 8), (1, 32))),
    }


masked_score = -1e+30

def attend_row(row_inputs):
    cache_keys, cache_values, length, query_rows, fresh_keys, fresh_values = row_inputs
    head_share = HEADS // KVH
    score_scale = HD ** (-0.5)
    query_wide = query_rows.astype(jnp.float32).reshape(STEPS, KVH, head_share, HD)
    keys_wide = cache_keys.astype(jnp.float32).reshape(CAP, KVH, HD)
    values_wide = cache_values.astype(jnp.float32).reshape(CAP, KVH, HD)
    fresh_keys_wide = fresh_keys.astype(jnp.float32).reshape(STEPS, KVH, HD)
    fresh_values_wide = fresh_values.astype(jnp.float32).reshape(STEPS, KVH, HD)
    usable = jnp.arange(CAP) < length
    cache_scores = jnp.einsum('sjgd,pjd->sjgp', query_wide, keys_wide) * score_scale
    cache_scores = jnp.where(usable, cache_scores, masked_score)
    causal = jnp.arange(STEPS)[:, None] >= jnp.arange(STEPS)[None, :]
    causal_mask = causal[:, None, None, :]
    fresh_scores = jnp.einsum('sjgd,tjd->sjgt', query_wide, fresh_keys_wide) * score_scale
    fresh_scores = jnp.where(causal_mask, fresh_scores, masked_score)
    ceiling = jnp.maximum(lax.optimization_barrier(jnp.max(cache_scores, axis=-1)), lax.optimization_barrier(jnp.max(fresh_scores, axis=-1)))
    cache_exp = jnp.where(usable, jnp.exp(cache_scores - ceiling[..., None]), 0.0)
    fresh_exp = jnp.where(causal_mask, jnp.exp(fresh_scores - ceiling[..., None]), 0.0)
    denominator = lax.optimization_barrier(jnp.sum(cache_exp, axis=-1)) + lax.optimization_barrier(jnp.sum(fresh_exp, axis=-1))
    cache_weights = lax.optimization_barrier(cache_exp.astype(jnp.bfloat16)).astype(jnp.float32)
    fresh_weights = lax.optimization_barrier(fresh_exp.astype(jnp.bfloat16)).astype(jnp.float32)
    weighted = jnp.einsum('sjgp,pjd->sjgd', cache_weights, values_wide)
    weighted = weighted + jnp.einsum('sjgt,tjd->sjgd', fresh_weights, fresh_values_wide)
    return (weighted / denominator[..., None]).reshape(STEPS, HEADS * HD)

def reference(key_cache, value_cache, lengths, queries, new_keys, new_values, residual, norm_gain, gate_weight, up_weight, down_weight):
    row_total = AGROUPS * GROUP_ROWS
    cache_keys = key_cache[:AGROUPS].reshape(row_total, CAP, KVH * HD)
    cache_values = value_cache[:AGROUPS].reshape(row_total, CAP, KVH * HD)
    row_lengths = lengths[:AGROUPS].reshape(row_total)
    query_rows = jnp.swapaxes(queries[:AGROUPS], 1, 2).reshape(row_total, STEPS, D)
    fresh_keys = jnp.swapaxes(new_keys[:AGROUPS], 1, 2).reshape(row_total, STEPS, KVH * HD)
    fresh_values = jnp.swapaxes(new_values[:AGROUPS], 1, 2).reshape(row_total, STEPS, KVH * HD)
    attended = lax.map(attend_row, (cache_keys, cache_values, row_lengths, query_rows, fresh_keys, fresh_values))
    attended = jnp.swapaxes(attended.reshape(AGROUPS, GROUP_ROWS, STEPS, D), 1, 2)
    hidden = residual[:AGROUPS].astype(jnp.float32) + attended
    spread_sq = lax.optimization_barrier(jnp.mean(hidden * hidden, axis=-1, keepdims=True))
    normed = (hidden * lax.rsqrt(spread_sq + 1e-05) * norm_gain).astype(jnp.bfloat16)
    flat_rows = normed.reshape(-1, D)
    numbers = (((1,), (1,)), ((), ()))
    gate_part = lax.dot_general(flat_rows, gate_weight[AGROUPS:].reshape(FF, D), numbers, preferred_element_type=jnp.float32)
    up_part = lax.dot_general(flat_rows, up_weight[AGROUPS:].reshape(FF, D), numbers, preferred_element_type=jnp.float32)
    product = (jax.nn.silu(gate_part) * up_part).astype(jnp.bfloat16)
    feed = jnp.dot(product, down_weight[AGROUPS:].reshape(FF, D), preferred_element_type=jnp.float32)
    mixed = (hidden + feed.reshape(hidden.shape)).astype(jnp.bfloat16)
    return jnp.concatenate([mixed, jnp.zeros_like(mixed)], axis=0)
```

```python
import jax
import jax.numpy as jnp
from jax import lax
from jax.sharding import Mesh
from jax.sharding import PartitionSpec as P

HEADS = 64
HD = 128
KVH = 4
X = ("xh", "xl")
GRP = ("y", "xh")
TP = ("z", "xl", "c")


masked_score = -1e30


def shifted(value, axes, hops):
    size = lax.axis_size(axes)
    return lax.ppermute(value, axes, [(i, (i + hops) % size) for i in range(size)])


def mirrored(value):
    return lax.ppermute(value, "y", [(i, 3 - i) for i in range(4)])


def opposite(value):
    return lax.ppermute(value, "y", [(i, (i + 2) % 4) for i in range(4)])


def gathered_rows(row):
    pair = jnp.concatenate([mirrored(row), opposite(row)], 0)
    planes, width = pair.shape
    depth = lax.axis_size("z")
    along_z = lax.all_to_all(
        jnp.broadcast_to(pair[None], (depth, planes, width)), "z", 0, 0, tiled=True
    ).reshape(depth * planes, width)
    near = [along_z] + [shifted(along_z, X, k) for k in (1, 2, 3)]
    half = jnp.concatenate(near, 0)
    return jnp.concatenate([half, shifted(half, "c", 1)], 0)


def returned_rows(partial):
    rows, width = partial.shape
    half = rows // 2
    other = shifted(partial[half:].astype(jnp.bfloat16), "c", 1)
    half_sum = partial[:half] + other.astype(jnp.float32)
    quarter = half // 4
    own = half_sum[:quarter]
    for k in (1, 2, 3):
        piece = half_sum[k * quarter : (k + 1) * quarter].astype(jnp.bfloat16)
        own = own + shifted(piece, X, -k).astype(jnp.float32)
    depth = lax.axis_size("z")
    pieces = own.astype(jnp.bfloat16).reshape(depth, quarter // depth, width)
    arrived = lax.all_to_all(pieces, "z", 0, 0, tiled=True)
    pair = jnp.sum(arrived.astype(jnp.float32), axis=0)
    return mirrored(pair[:1]) + opposite(pair[1:])


def feed_rows(normed_rows, gate_weight, up_weight, down_weight):
    numbers = (((1,), (1,)), ((), ()))
    gate_part = lax.dot_general(
        normed_rows, gate_weight[0], numbers, preferred_element_type=jnp.float32
    )
    up_part = lax.dot_general(
        normed_rows, up_weight[0], numbers, preferred_element_type=jnp.float32
    )
    product = (jax.nn.silu(gate_part) * up_part).astype(jnp.bfloat16)
    return jnp.dot(product, down_weight[0], preferred_element_type=jnp.float32)


def local(
    key_cache,
    value_cache,
    lengths,
    queries,
    new_keys,
    new_values,
    residual,
    norm_gain,
    gate_weight,
    up_weight,
    down_weight,
):
    serving = lax.axis_index("y") < lax.axis_size("y") // 2
    step_count = queries.shape[1]
    own_rows = queries.shape[2]
    model_width = queries.shape[3]
    head_share = HEADS // KVH
    slot_count = key_cache.shape[2]
    score_scale = HD ** (-0.5)
    own_heads = queries[0].reshape(step_count, own_rows, KVH, head_share, HD)
    cache_keys = key_cache[0].reshape(own_rows, slot_count, KVH, HD)
    cache_values = value_cache[0].reshape(own_rows, slot_count, KVH, HD)
    positions = jnp.arange(slot_count)
    usable = positions[None, :] < lengths[0][:, None]
    usable_mask = usable[None, :, None, None, :]
    cache_scores = (
        jnp.einsum("srjgd,rpjd->srjgp", own_heads, cache_keys, preferred_element_type=jnp.float32)
        * score_scale
    )
    cache_scores = jnp.where(usable_mask, cache_scores, masked_score)
    fresh_keys = new_keys[0].reshape(step_count, own_rows, KVH, HD)
    fresh_values = new_values[0].reshape(step_count, own_rows, KVH, HD)
    fresh_scores = (
        jnp.einsum("srjgd,trjd->srjgt", own_heads, fresh_keys, preferred_element_type=jnp.float32)
        * score_scale
    )
    causal = jnp.arange(step_count)[:, None] >= jnp.arange(step_count)[None, :]
    causal_mask = causal[:, None, None, None, :]
    fresh_scores = jnp.where(causal_mask, fresh_scores, masked_score)
    ceiling = jnp.maximum(jnp.max(cache_scores, axis=-1), jnp.max(fresh_scores, axis=-1))
    cache_exp = jnp.where(usable_mask, jnp.exp(cache_scores - ceiling[..., None]), 0.0)
    fresh_exp = jnp.where(causal_mask, jnp.exp(fresh_scores - ceiling[..., None]), 0.0)
    denominator = jnp.sum(cache_exp, axis=-1) + jnp.sum(fresh_exp, axis=-1)
    cache_weighted = jnp.einsum(
        "srjgp,rpjd->srjgd",
        cache_exp.astype(jnp.bfloat16),
        cache_values,
        preferred_element_type=jnp.float32,
    )
    fresh_weighted = jnp.einsum(
        "srjgt,trjd->srjgd",
        fresh_exp.astype(jnp.bfloat16),
        fresh_values,
        preferred_element_type=jnp.float32,
    )
    attended = (cache_weighted + fresh_weighted) / denominator[..., None]
    attended = attended.reshape(step_count, own_rows, model_width)
    hidden = residual[0].astype(jnp.float32) + attended
    spread_sq = jnp.mean(hidden * hidden, axis=-1, keepdims=True)
    normed = (hidden * lax.rsqrt(spread_sq + 1e-05) * norm_gain).astype(jnp.bfloat16)
    flat_rows = normed.reshape(step_count * own_rows, model_width)
    all_rows = gathered_rows(flat_rows)
    summed = returned_rows(feed_rows(all_rows, gate_weight, up_weight, down_weight))
    mixed = (hidden + summed.reshape(step_count, own_rows, model_width)).astype(jnp.bfloat16)
    mixed = jnp.where(serving, mixed, jnp.zeros_like(mixed))
    return mixed[None]


def solution(mesh):
    finer = Mesh(mesh.devices.reshape(4, 2, 8, 2, 2), ("y", "xh", "z", "xl", "c"))
    in_specs = (
        P(GRP, TP, None, None),
        P(GRP, TP, None, None),
        P(GRP, TP),
        P(GRP, None, TP, None),
        P(GRP, None, TP, None),
        P(GRP, None, TP, None),
        P(GRP, None, TP, None),
        P(),
        P(GRP, TP, None),
        P(GRP, TP, None),
        P(GRP, TP, None),
    )
    out_specs = P(GRP, None, TP, None)
    return jax.shard_map(local, mesh=finer, in_specs=in_specs, out_specs=out_specs, check_vma=False)
```

```python
import jax
import jax.numpy as jnp
from jax import lax
from jax.experimental import pallas as pl
from jax.experimental.pallas import tpu as pltpu
from jax.sharding import Mesh
from jax.sharding import PartitionSpec as P

HEADS = 64
HD = 128
KVH = 4
X = ("xh", "xl")
GRP = ("y", "xh")
TP = ("z", "xl", "c")


masked_score = -1e30


def shifted(value, axes, hops):
    size = lax.axis_size(axes)
    return lax.ppermute(value, axes, [(i, (i + hops) % size) for i in range(size)])


def swapped(value):
    return shifted(value, "c", 1)


def mirrored(value):
    return lax.ppermute(value, "y", [(i, 3 - i) for i in range(4)])


def opposite(value):
    return lax.ppermute(value, "y", [(i, (i + 2) % 4) for i in range(4)])


def in_hbm(value):
    return pltpu.with_memory_space_constraint(value, pltpu.HBM)


def wide(value):
    return value.astype(jnp.float32)


def narrow(value):
    return value.astype(jnp.bfloat16)


def pairs_kernel(pairs_ref, first_ref, second_ref):
    for i in range(4):
        first_ref[pl.ds(2 * i, 2), :] = pairs_ref[i]
        second_ref[pl.ds(2 * i, 2), :] = pairs_ref[4 + i]


def rows_of_pairs(pairs):
    half = pltpu.VMEM((8, pairs.shape[-1]), pairs.dtype)
    in_vmem = pl.BlockSpec(memory_space=pltpu.VMEM)
    return pl.pallas_call(
        pairs_kernel, out_shape=(half, half), in_specs=[in_vmem], out_specs=(in_vmem, in_vmem)
    )(pairs)


def gathered_blocks(row):
    pair = jnp.concatenate([mirrored(row), opposite(row)], 0)
    planes, width = pair.shape
    depth = lax.axis_size("z")
    pairs = lax.all_to_all(
        jnp.broadcast_to(pair[None], (depth, planes, width)), "z", 0, 0, tiled=True
    )
    first, second = rows_of_pairs(pairs)
    low = shifted(first, X, 1)
    high = shifted(second, X, -1)
    low_rest = shifted(second, X, 1)
    high_rest = shifted(first, X, -1)
    low_far = shifted(low, X, 1)
    high_far = shifted(high, X, -1)
    blocks = [first, second, low, low_rest, high_rest, high, low_far, high_far]
    return blocks + [swapped(b) for b in blocks]


def returned_rows(keep, send):
    total = keep + wide(swapped(send))
    own = total[:16]
    near_low, near_high, far = total[16:32], total[32:48], total[48:]
    far_low = shifted(narrow(far[:8]), X, -1)
    far_high = shifted(narrow(far[8:]), X, 1)
    low_rest = shifted(narrow(near_low[8:]), X, -1)
    high_rest = shifted(narrow(near_high[:8]), X, 1)
    low = shifted(narrow(near_low[:8] + wide(far_low)), X, -1)
    high = shifted(narrow(near_high[8:] + wide(far_high)), X, 1)
    first = own[:8] + wide(high_rest) + wide(low)
    second = own[8:] + wide(low_rest) + wide(high)
    own = jnp.concatenate([narrow(first), narrow(second)], 0)
    depth = lax.axis_size("z")
    pieces = own.reshape(depth, 2, own.shape[-1])
    arrived = lax.all_to_all(pieces, "z", 0, 0, tiled=True)
    pair = jnp.sum(arrived.astype(jnp.float32), axis=0)
    return mirrored(pair[:1]) + opposite(pair[1:])


CHUNKS = 4


def feed_kernel(*refs):
    blocks, rest = refs[:16], refs[16:]
    gate_hbm, up_hbm, down_hbm, keep_ref, send_ref, rows_ref, gate_ref, up_ref, down_ref, row_sems, sems = rest
    width = rows_ref.shape[1]
    part = width // CHUNKS
    row_copies = []
    for i, block in enumerate(blocks):
        size = block.shape[0]
        row_copies.append(
            pltpu.make_async_copy(block, rows_ref.at[pl.ds(i * size, size)], row_sems.at[i])
        )
    weight_copies = []
    for k in range(CHUNKS):
        for w, (hbm, vmem) in enumerate(((gate_hbm, gate_ref), (up_hbm, up_ref))):
            columns = pl.ds(k * part, part)
            weight_copies.append(
                pltpu.make_async_copy(hbm.at[:, columns], vmem.at[:, columns], sems.at[2 * k + w])
            )
    down_copy = pltpu.make_async_copy(down_hbm, down_ref, sems.at[2 * CHUNKS])
    for copy in row_copies + weight_copies + [down_copy]:
        copy.start()
    for copy in row_copies:
        copy.wait()
    numbers = (((1,), (1,)), ((), ()))
    gate = jnp.zeros((rows_ref.shape[0], gate_ref.shape[0]), jnp.float32)
    up = gate
    for k in range(CHUNKS):
        columns = pl.ds(k * part, part)
        rows = rows_ref[:, columns]
        weight_copies[2 * k].wait()
        gate = gate + lax.dot_general(rows, gate_ref[:, columns], numbers, preferred_element_type=jnp.float32)
        weight_copies[2 * k + 1].wait()
        up = up + lax.dot_general(rows, up_ref[:, columns], numbers, preferred_element_type=jnp.float32)
    act = (gate / (1.0 + jnp.exp(-gate)) * up).astype(jnp.bfloat16)
    down_copy.wait()
    half = rows_ref.shape[0] // 2
    send_ref[...] = jnp.dot(act[half:], down_ref[...], preferred_element_type=jnp.float32).astype(jnp.bfloat16)
    keep_ref[...] = jnp.dot(act[:half], down_ref[...], preferred_element_type=jnp.float32)


def feed_rows(blocks, gate_weight, up_weight, down_weight):
    units, width = gate_weight.shape[1:]
    anywhere = pl.BlockSpec(memory_space=pl.ANY)
    in_vmem = pl.BlockSpec(memory_space=pltpu.VMEM)
    held = pltpu.VMEM((units, width), jnp.bfloat16)
    return pl.pallas_call(
        feed_kernel,
        out_shape=(
            jax.ShapeDtypeStruct((64, width), jnp.float32),
            jax.ShapeDtypeStruct((64, width), jnp.bfloat16),
        ),
        in_specs=[anywhere] * len(blocks) + [pl.BlockSpec(memory_space=pltpu.HBM)] * 3,
        out_specs=(in_vmem, in_vmem),
        scratch_shapes=[
            pltpu.VMEM((128, width), jnp.bfloat16),
            held,
            held,
            held,
            pltpu.SemaphoreType.DMA((16,)),
            pltpu.SemaphoreType.DMA((2 * CHUNKS + 1,)),
        ],
        compiler_params=pltpu.CompilerParams(vmem_limit_bytes=28 << 20),
    )(*blocks, *(in_hbm(w[0]) for w in (gate_weight, up_weight, down_weight)))


def attend_kernel(
    length_ref,
    key_hbm,
    value_hbm,
    query_hbm,
    fresh_key_hbm,
    fresh_value_hbm,
    residual_hbm,
    gain_hbm,
    hidden_ref,
    normed_ref,
    keys,
    values,
    query,
    fresh_key,
    fresh_value,
    residual,
    gain,
    query_rows,
    residual_rows,
    sems,
):
    sources = (query_hbm, key_hbm, fresh_key_hbm, value_hbm, fresh_value_hbm, residual_hbm, gain_hbm)
    targets = (query, keys, fresh_key, values, fresh_value, residual, gain)
    copies = [pltpu.make_async_copy(s, t, sems.at[i]) for i, (s, t) in enumerate(zip(sources, targets))]
    for copy in copies:
        copy.start()
    copies[0].wait()
    for h in range(HEADS):
        query_rows[pl.ds(h, 1), :] = query[:, pl.ds(h * HD, HD)].astype(jnp.float32)
    slots = keys.shape[0]
    share = HEADS // KVH
    scale = HD ** (-0.5)
    usable = lax.broadcasted_iota(jnp.int32, (share, slots), 1) < length_ref[0, 0]
    copies[1].wait()
    copies[2].wait()
    weights = []
    for j in range(KVH):
        wide_query = query_rows[pl.ds(j * share, share), :]
        lanes = pl.ds(j * HD, HD)
        scores = lax.dot_general(
            wide_query.astype(jnp.bfloat16),
            keys[:, lanes],
            (((1,), (1,)), ((), ())),
            preferred_element_type=jnp.float32,
        )
        scores = jnp.where(usable, scores * scale, masked_score)
        fresh = jnp.sum(wide_query * fresh_key[:, lanes].astype(jnp.float32), axis=-1, keepdims=True) * scale
        ceiling = jnp.maximum(jnp.max(scores, axis=-1, keepdims=True), fresh)
        expo = jnp.where(usable, jnp.exp(scores - ceiling), 0.0)
        fresh_expo = jnp.exp(fresh - ceiling)
        denominator = jnp.sum(expo, axis=-1, keepdims=True) + fresh_expo
        weights.append((expo.astype(jnp.bfloat16), fresh_expo.astype(jnp.bfloat16), denominator))
    for copy in copies[3:]:
        copy.wait()
    for h in range(HEADS):
        residual_rows[pl.ds(h, 1), :] = residual[:, pl.ds(h * HD, HD)].astype(jnp.float32)
    square = jnp.zeros((1, 1), jnp.float32)
    for j in range(KVH):
        lanes = pl.ds(j * HD, HD)
        rows = pl.ds(j * share, share)
        expo, fresh_expo, denominator = weights[j]
        weighted = jnp.dot(expo, values[:, lanes], preferred_element_type=jnp.float32)
        weighted = weighted + fresh_expo.astype(jnp.float32) * fresh_value[:, lanes].astype(jnp.float32)
        hidden = residual_rows[rows, :] + weighted / denominator
        residual_rows[rows, :] = hidden
        square = square + jnp.sum(jnp.sum(hidden * hidden, axis=-1, keepdims=True), axis=0, keepdims=True)
    factor = lax.rsqrt(square / (HEADS * HD) + 1e-05)
    query_rows[...] = residual_rows[...] * factor * gain[...]
    for h in range(HEADS):
        lanes = pl.ds(h * HD, HD)
        hidden_ref[:, lanes] = residual_rows[pl.ds(h, 1), :]
        normed_ref[:, lanes] = query_rows[pl.ds(h, 1), :].astype(jnp.bfloat16)


def attend(lengths, key_cache, value_cache, queries, new_keys, new_values, residual, norm_gain):
    slots, columns = key_cache.shape[2:]
    width = queries.shape[-1]
    cache = (slots, columns)
    args = (
        lengths,
        key_cache.reshape(cache),
        value_cache.reshape(cache),
        queries.reshape(1, width),
        new_keys.reshape(1, columns),
        new_values.reshape(1, columns),
        residual.reshape(1, width),
        norm_gain.reshape(HEADS, HD),
    )
    in_vmem = pl.BlockSpec(memory_space=pltpu.VMEM)
    rows = pltpu.VMEM((HEADS, HD), jnp.float32)
    return pl.pallas_call(
        attend_kernel,
        out_shape=(
            jax.ShapeDtypeStruct((1, width), jnp.float32),
            jax.ShapeDtypeStruct((1, width), jnp.bfloat16),
        ),
        in_specs=[pl.BlockSpec(memory_space=pltpu.SMEM)] + [pl.BlockSpec(memory_space=pltpu.HBM)] * 7,
        out_specs=(in_vmem, in_vmem),
        scratch_shapes=[
            pltpu.VMEM(cache, jnp.bfloat16),
            pltpu.VMEM(cache, jnp.bfloat16),
            pltpu.VMEM((1, width), jnp.bfloat16),
            pltpu.VMEM((1, columns), jnp.bfloat16),
            pltpu.VMEM((1, columns), jnp.bfloat16),
            pltpu.VMEM((1, width), jnp.bfloat16),
            rows,
            rows,
            rows,
            pltpu.SemaphoreType.DMA((7,)),
        ],
        compiler_params=pltpu.CompilerParams(vmem_limit_bytes=16 << 20),
    )(args[0], *(in_hbm(arg) for arg in args[1:]))


def local(
    key_cache,
    value_cache,
    lengths,
    queries,
    new_keys,
    new_values,
    residual,
    norm_gain,
    gate_weight,
    up_weight,
    down_weight,
):
    serving = lax.axis_index("y") < lax.axis_size("y") // 2
    hidden, flat_rows = attend(
        lengths, key_cache, value_cache, queries, new_keys, new_values, residual, norm_gain
    )
    keep, send = feed_rows(gathered_blocks(flat_rows), gate_weight, up_weight, down_weight)
    summed = returned_rows(keep, send)
    mixed = (hidden + summed).astype(jnp.bfloat16)
    mixed = jnp.where(serving, mixed, jnp.zeros_like(mixed))
    return mixed.reshape(residual.shape)


def solution(mesh):
    finer = Mesh(mesh.devices.reshape(4, 2, 8, 2, 2), ("y", "xh", "z", "xl", "c"))
    in_specs = (
        P(GRP, TP, None, None),
        P(GRP, TP, None, None),
        P(GRP, TP),
        P(GRP, None, TP, None),
        P(GRP, None, TP, None),
        P(GRP, None, TP, None),
        P(GRP, None, TP, None),
        P(),
        P(GRP, TP, None),
        P(GRP, TP, None),
        P(GRP, TP, None),
    )
    out_specs = P(GRP, None, TP, None)
    return jax.shard_map(local, mesh=finer, in_specs=in_specs, out_specs=out_specs, check_vma=False)
```

```python
import functools

import jax
import jax.numpy as jnp
from jax import lax
from jax.experimental import pallas as pl
from jax.experimental.pallas import tpu as pltpu
from jax.sharding import Mesh
from jax.sharding import PartitionSpec as P

HEADS = 64
HD = 128
KVH = 4
X = ("xh", "xl")
GRP = ("y", "xh")
TP = ("z", "xl", "c")


masked_score = -1e30


def shifted(value, axes, hops):
    size = lax.axis_size(axes)
    return lax.ppermute(value, axes, [(i, (i + hops) % size) for i in range(size)])


def swapped(value):
    return shifted(value, "c", 1)


def mirrored(value):
    return lax.ppermute(value, "y", [(i, 3 - i) for i in range(4)])


def opposite(value):
    return lax.ppermute(value, "y", [(i, (i + 2) % 4) for i in range(4)])


def in_hbm(value):
    return pltpu.with_memory_space_constraint(value, pltpu.HBM)


def wide(value):
    return value.astype(jnp.float32)


def narrow(value):
    return value.astype(jnp.bfloat16)


def spread_kernel(near_ref, far_ref, copies_ref):
    near, far = near_ref[...], far_ref[...]
    for i in range(copies_ref.shape[0]):
        copies_ref[i, pl.ds(0, 1), :] = near
        copies_ref[i, pl.ds(1, 1), :] = far


def spread(near, far):
    in_vmem = pl.BlockSpec(memory_space=pltpu.VMEM)
    return pl.pallas_call(
        spread_kernel,
        out_shape=pltpu.VMEM((8, 2, near.shape[-1]), near.dtype),
        in_specs=[in_vmem, in_vmem],
        out_specs=in_vmem,
        compiler_params=pltpu.CompilerParams(vmem_limit_bytes=4 << 20),
    )(near, far)


def pairs_kernel(pairs_ref, rows_ref):
    for i in range(pairs_ref.shape[0]):
        rows_ref[pl.ds(2 * i, 2), :] = pairs_ref[i]


def rows_of_pairs(pairs):
    count, _, width = pairs.shape
    in_vmem = pl.BlockSpec(memory_space=pltpu.VMEM)
    return pl.pallas_call(
        pairs_kernel,
        out_shape=pltpu.VMEM((2 * count, width), pairs.dtype),
        in_specs=[in_vmem],
        out_specs=in_vmem,
        compiler_params=pltpu.CompilerParams(vmem_limit_bytes=4 << 20),
    )(pairs)


def half_kernel(block_ref, token_ref, half_ref, *, start):
    half_ref[...] = block_ref[pl.ds(start, half_ref.shape[0]), :]


def half_of(block, start, token):
    rows, width = block.shape
    in_vmem = pl.BlockSpec(memory_space=pltpu.VMEM)
    return pl.pallas_call(
        functools.partial(half_kernel, start=start),
        out_shape=pltpu.VMEM((rows // 2, width), block.dtype),
        in_specs=[in_vmem, pl.BlockSpec(memory_space=pl.ANY)],
        out_specs=in_vmem,
        compiler_params=pltpu.CompilerParams(vmem_limit_bytes=4 << 20),
    )(block, token)


def gathered_blocks(row, weights):
    copies = spread(mirrored(row), opposite(row))
    pairs = lax.all_to_all(copies, "z", 0, 0, tiled=True)
    block = rows_of_pairs(pairs)
    *weights, token = loaded(weights, block)
    low = shifted(block, X, 1)
    high = shifted(block, X, -1)
    low_far = shifted(half_of(low, 0, token), X, 1)
    high_far = shifted(half_of(high, 8, token), X, -1)
    blocks = [block, low, high, low_far, high_far]
    return blocks + [swapped(b) for b in blocks], weights


def returned_rows(keep, send):
    total = keep + wide(swapped(send))
    own = total[:16]
    near_low, near_high, far = total[16:32], total[32:48], total[48:]
    far_low = shifted(narrow(far[:8]), X, -1)
    far_high = shifted(narrow(far[8:]), X, 1)
    low_rest = shifted(narrow(near_low[8:]), X, -1)
    high_rest = shifted(narrow(near_high[:8]), X, 1)
    low = shifted(narrow(near_low[:8] + wide(far_low)), X, -1)
    high = shifted(narrow(near_high[8:] + wide(far_high)), X, 1)
    first = own[:8] + wide(high_rest) + wide(low)
    second = own[8:] + wide(low_rest) + wide(high)
    own = jnp.concatenate([narrow(first), narrow(second)], 0)
    depth = lax.axis_size("z")
    pieces = own.reshape(depth, 2, own.shape[-1])
    arrived = lax.all_to_all(pieces, "z", 0, 0, tiled=True)
    pair = jnp.sum(arrived.astype(jnp.float32), axis=0)
    return mirrored(pair[:1]) + opposite(pair[1:])


def load_kernel(*refs):
    sources, targets, token_ref, sems = refs[:3], refs[4:7], refs[7], refs[8]
    copies = []
    parts = 2
    for w, (source, target) in enumerate(zip(sources, targets)):
        size = source.shape[0] // parts
        for i in range(parts):
            rows = pl.ds(i * size, size)
            copies.append(pltpu.make_async_copy(source.at[rows], target.at[rows], sems.at[w * parts + i]))
    for copy in copies:
        copy.start()
    token_ref[...] = jnp.zeros_like(token_ref)
    for copy in copies:
        copy.wait()


def loaded(weights, rows):
    in_vmem = pl.BlockSpec(memory_space=pltpu.VMEM)
    return pl.pallas_call(
        load_kernel,
        out_shape=tuple(pltpu.VMEM(w.shape, w.dtype) for w in weights) + (pltpu.VMEM((8, 128), jnp.float32),),
        in_specs=[pl.BlockSpec(memory_space=pltpu.HBM)] * 3 + [pl.BlockSpec(memory_space=pl.ANY)],
        out_specs=(in_vmem,) * 4,
        scratch_shapes=[pltpu.SemaphoreType.DMA((6,))],
        compiler_params=pltpu.CompilerParams(vmem_limit_bytes=12 << 20),
    )(*(in_hbm(w) for w in weights), rows)


def feed_kernel(*refs):
    blocks, (gate_ref, up_ref, down_ref, keep_ref, send_ref, rows_ref) = refs[:-6], refs[-6:]
    at = 0
    for block in blocks:
        size = block.shape[0]
        rows_ref[pl.ds(at, size), :] = block[...]
        at += size
    rows = rows_ref[...]
    numbers = (((1,), (1,)), ((), ()))
    gate = lax.dot_general(gate_ref[...], rows, numbers, preferred_element_type=jnp.float32)
    up = lax.dot_general(up_ref[...], rows, numbers, preferred_element_type=jnp.float32)
    act = (gate / (1.0 + jnp.exp(-gate)) * up).T.astype(jnp.bfloat16)
    half = at // 2
    part = 1024
    for k in range(rows_ref.shape[1] // part):
        columns = pl.ds(k * part, part)
        feed = jnp.dot(act, down_ref[:, columns], preferred_element_type=jnp.float32)
        keep_ref[:, columns] = feed[:half]
        send_ref[:, columns] = feed[half:].astype(jnp.bfloat16)


def feed_rows(blocks, weights):
    width = weights[0].shape[-1]
    in_vmem = pl.BlockSpec(memory_space=pltpu.VMEM)
    held = [pltpu.with_memory_space_constraint(w, pltpu.VMEM) for w in weights]
    return pl.pallas_call(
        feed_kernel,
        out_shape=(
            pltpu.VMEM((64, width), jnp.float32),
            pltpu.VMEM((64, width), jnp.bfloat16),
        ),
        in_specs=[in_vmem] * (len(blocks) + 3),
        out_specs=(in_vmem, in_vmem),
        scratch_shapes=[pltpu.VMEM((128, width), jnp.bfloat16)],
        compiler_params=pltpu.CompilerParams(vmem_limit_bytes=12 << 20),
    )(*blocks, *held)


def attend_kernel(
    length_ref,
    key_hbm,
    value_hbm,
    query_hbm,
    fresh_key_hbm,
    fresh_value_hbm,
    residual_hbm,
    gain_hbm,
    hidden_ref,
    normed_ref,
    keys,
    values,
    query,
    fresh_key,
    fresh_value,
    residual,
    gain,
    query_rows,
    residual_rows,
    sems,
):
    sources = (query_hbm, key_hbm, fresh_key_hbm, value_hbm, fresh_value_hbm, residual_hbm, gain_hbm)
    targets = (query, keys, fresh_key, values, fresh_value, residual, gain)
    copies = [pltpu.make_async_copy(s, t, sems.at[i]) for i, (s, t) in enumerate(zip(sources, targets))]
    for copy in copies:
        copy.start()
    copies[0].wait()
    for h in range(HEADS):
        query_rows[pl.ds(h, 1), :] = query[:, pl.ds(h * HD, HD)].astype(jnp.float32)
    slots = keys.shape[0]
    share = HEADS // KVH
    scale = HD ** (-0.5)
    usable = lax.broadcasted_iota(jnp.int32, (share, slots), 1) < length_ref[0, 0]
    copies[1].wait()
    copies[2].wait()
    weights = []
    for j in range(KVH):
        wide_query = query_rows[pl.ds(j * share, share), :]
        lanes = pl.ds(j * HD, HD)
        scores = lax.dot_general(
            wide_query.astype(jnp.bfloat16),
            keys[:, lanes],
            (((1,), (1,)), ((), ())),
            preferred_element_type=jnp.float32,
        )
        scores = jnp.where(usable, scores * scale, masked_score)
        fresh = jnp.sum(wide_query * fresh_key[:, lanes].astype(jnp.float32), axis=-1, keepdims=True) * scale
        ceiling = jnp.maximum(jnp.max(scores, axis=-1, keepdims=True), fresh)
        expo = jnp.where(usable, jnp.exp(scores - ceiling), 0.0)
        fresh_expo = jnp.exp(fresh - ceiling)
        denominator = jnp.sum(expo, axis=-1, keepdims=True) + fresh_expo
        weights.append((expo.astype(jnp.bfloat16), fresh_expo.astype(jnp.bfloat16), denominator))
    for copy in copies[3:]:
        copy.wait()
    for h in range(HEADS):
        residual_rows[pl.ds(h, 1), :] = residual[:, pl.ds(h * HD, HD)].astype(jnp.float32)
    square = jnp.zeros((1, 1), jnp.float32)
    for j in range(KVH):
        lanes = pl.ds(j * HD, HD)
        rows = pl.ds(j * share, share)
        expo, fresh_expo, denominator = weights[j]
        weighted = jnp.dot(expo, values[:, lanes], preferred_element_type=jnp.float32)
        weighted = weighted + fresh_expo.astype(jnp.float32) * fresh_value[:, lanes].astype(jnp.float32)
        hidden = residual_rows[rows, :] + weighted / denominator
        residual_rows[rows, :] = hidden
        square = square + jnp.sum(jnp.sum(hidden * hidden, axis=-1, keepdims=True), axis=0, keepdims=True)
    factor = lax.rsqrt(square / (HEADS * HD) + 1e-05)
    query_rows[...] = residual_rows[...] * factor * gain[...]
    for h in range(HEADS):
        lanes = pl.ds(h * HD, HD)
        hidden_ref[:, lanes] = residual_rows[pl.ds(h, 1), :]
        normed_ref[:, lanes] = query_rows[pl.ds(h, 1), :].astype(jnp.bfloat16)


def attend(lengths, key_cache, value_cache, queries, new_keys, new_values, residual, norm_gain):
    slots, columns = key_cache.shape[2:]
    width = queries.shape[-1]
    cache = (slots, columns)
    args = (
        lengths,
        key_cache.reshape(cache),
        value_cache.reshape(cache),
        queries.reshape(1, width),
        new_keys.reshape(1, columns),
        new_values.reshape(1, columns),
        residual.reshape(1, width),
        norm_gain.reshape(HEADS, HD),
    )
    in_vmem = pl.BlockSpec(memory_space=pltpu.VMEM)
    rows = pltpu.VMEM((HEADS, HD), jnp.float32)
    return pl.pallas_call(
        attend_kernel,
        out_shape=(
            jax.ShapeDtypeStruct((1, width), jnp.float32),
            jax.ShapeDtypeStruct((1, width), jnp.bfloat16),
        ),
        in_specs=[pl.BlockSpec(memory_space=pltpu.SMEM)] + [pl.BlockSpec(memory_space=pltpu.HBM)] * 7,
        out_specs=(in_vmem, in_vmem),
        scratch_shapes=[
            pltpu.VMEM(cache, jnp.bfloat16),
            pltpu.VMEM(cache, jnp.bfloat16),
            pltpu.VMEM((1, width), jnp.bfloat16),
            pltpu.VMEM((1, columns), jnp.bfloat16),
            pltpu.VMEM((1, columns), jnp.bfloat16),
            pltpu.VMEM((1, width), jnp.bfloat16),
            rows,
            rows,
            rows,
            pltpu.SemaphoreType.DMA((7,)),
        ],
        compiler_params=pltpu.CompilerParams(vmem_limit_bytes=16 << 20),
    )(args[0], *(in_hbm(arg) for arg in args[1:]))


def local(
    key_cache,
    value_cache,
    lengths,
    queries,
    new_keys,
    new_values,
    residual,
    norm_gain,
    gate_weight,
    up_weight,
    down_weight,
):
    serving = lax.axis_index("y") < lax.axis_size("y") // 2
    hidden, flat_rows = attend(
        lengths, key_cache, value_cache, queries, new_keys, new_values, residual, norm_gain
    )
    weights = gate_weight[0], up_weight[0], down_weight[0]
    keep, send = feed_rows(*gathered_blocks(flat_rows, weights))
    summed = returned_rows(keep, send)
    mixed = (hidden + summed).astype(jnp.bfloat16)
    mixed = jnp.where(serving, mixed, jnp.zeros_like(mixed))
    return mixed.reshape(residual.shape)


def solution(mesh):
    finer = Mesh(mesh.devices.reshape(4, 2, 8, 2, 2), ("y", "xh", "z", "xl", "c"))
    in_specs = (
        P(GRP, TP, None, None),
        P(GRP, TP, None, None),
        P(GRP, TP),
        P(GRP, None, TP, None),
        P(GRP, None, TP, None),
        P(GRP, None, TP, None),
        P(GRP, None, TP, None),
        P(),
        P(GRP, TP, None),
        P(GRP, TP, None),
        P(GRP, TP, None),
    )
    out_specs = P(GRP, None, TP, None)
    return jax.shard_map(local, mesh=finer, in_specs=in_specs, out_specs=out_specs, check_vma=False)
```

```python
import functools

import jax
import jax.numpy as jnp
from jax import lax
from jax.experimental import pallas as pl
from jax.experimental.pallas import tpu as pltpu
from jax.sharding import Mesh
from jax.sharding import PartitionSpec as P

HEADS = 64
HD = 128
KVH = 4
X = ("xh", "xl")
GRP = ("y", "xh")
TP = ("z", "xl", "c")


masked_score = -1e30


def shifted(value, axes, hops):
    size = lax.axis_size(axes)
    return lax.ppermute(value, axes, [(i, (i + hops) % size) for i in range(size)])


def swapped(value):
    return shifted(value, "c", 1)


def mirrored(value):
    return lax.ppermute(value, "y", [(i, 3 - i) for i in range(4)])


def opposite(value):
    return lax.ppermute(value, "y", [(i, (i + 2) % 4) for i in range(4)])


def in_hbm(value):
    return pltpu.with_memory_space_constraint(value, pltpu.HBM)


def wide(value):
    return value.astype(jnp.float32)


def narrow(value):
    return value.astype(jnp.bfloat16)


def spread_kernel(near_ref, far_ref, copies_ref):
    near, far = near_ref[...], far_ref[...]
    for i in range(copies_ref.shape[0]):
        copies_ref[i, pl.ds(0, 1), :] = near
        copies_ref[i, pl.ds(1, 1), :] = far


def spread(near, far):
    in_vmem = pl.BlockSpec(memory_space=pltpu.VMEM)
    return pl.pallas_call(
        spread_kernel,
        out_shape=pltpu.VMEM((8, 2, near.shape[-1]), near.dtype),
        in_specs=[in_vmem, in_vmem],
        out_specs=in_vmem,
        compiler_params=pltpu.CompilerParams(vmem_limit_bytes=4 << 20),
    )(near, far)


def pairs_kernel(pairs_ref, rows_ref):
    for i in range(pairs_ref.shape[0]):
        rows_ref[pl.ds(2 * i, 2), :] = pairs_ref[i]


def rows_of_pairs(pairs):
    count, _, width = pairs.shape
    in_vmem = pl.BlockSpec(memory_space=pltpu.VMEM)
    return pl.pallas_call(
        pairs_kernel,
        out_shape=pltpu.VMEM((2 * count, width), pairs.dtype),
        in_specs=[in_vmem],
        out_specs=in_vmem,
        compiler_params=pltpu.CompilerParams(vmem_limit_bytes=4 << 20),
    )(pairs)


def half_kernel(block_ref, token_ref, half_ref, *, start):
    half_ref[...] = block_ref[pl.ds(start, half_ref.shape[0]), :]


def half_of(block, start, token):
    rows, width = block.shape
    in_vmem = pl.BlockSpec(memory_space=pltpu.VMEM)
    return pl.pallas_call(
        functools.partial(half_kernel, start=start),
        out_shape=pltpu.VMEM((rows // 2, width), block.dtype),
        in_specs=[in_vmem, pl.BlockSpec(memory_space=pl.ANY)],
        out_specs=in_vmem,
        compiler_params=pltpu.CompilerParams(vmem_limit_bytes=4 << 20),
    )(block, token)


def along_x(value, hops):
    pairs = [(x * 2 + c, (x + (1 - 2 * c) * hops) % 4 * 2 + c) for x in range(4) for c in range(2)]
    return lax.ppermute(value, X + ("c",), pairs)


def gathered_blocks(row, weights):
    copies = spread(mirrored(row), opposite(row))
    pairs = lax.all_to_all(copies, "z", 0, 0, tiled=True)
    block = rows_of_pairs(pairs)
    *weights, token = loaded(weights, block)
    near = along_x(block, 1)
    back = along_x(block, -1)
    far_low = along_x(half_of(near, 0, token), 1)
    far_high = along_x(half_of(back, 8, token), -1)
    kept = [block, near, swapped(back), far_low, far_high]
    return kept + [swapped(block), swapped(near), back, swapped(far_low), swapped(far_high)], weights


def returned_rows(keep, send, send_far):
    far = keep[48:] + wide(swapped(send_far))
    rest = keep[:48] + wide(swapped(send))
    own, near, near_other = rest[:16], rest[16:32], rest[32:]
    far_in = along_x(narrow(far), -1)
    other_in = along_x(narrow(near_other), -1)
    near_in = along_x(narrow(near + wide(far_in)), -1)
    own = narrow(own + wide(swapped(other_in)) + wide(near_in))
    depth = lax.axis_size("z")
    pieces = own.reshape(depth, 2, own.shape[-1])
    arrived = lax.all_to_all(pieces, "z", 0, 0, tiled=True)
    pair = jnp.sum(arrived.astype(jnp.float32), axis=0)
    return mirrored(pair[:1]) + opposite(pair[1:])


def load_kernel(*refs):
    sources, targets, token_ref, sems = refs[:3], refs[4:7], refs[7], refs[8]
    copies = []
    parts = 2
    for w, (source, target) in enumerate(zip(sources, targets)):
        size = source.shape[0] // parts
        for i in range(parts):
            rows = pl.ds(i * size, size)
            copies.append(pltpu.make_async_copy(source.at[rows], target.at[rows], sems.at[w * parts + i]))
    for copy in copies:
        copy.start()
    token_ref[...] = jnp.zeros_like(token_ref)
    for copy in copies:
        copy.wait()


def loaded(weights, rows):
    in_vmem = pl.BlockSpec(memory_space=pltpu.VMEM)
    return pl.pallas_call(
        load_kernel,
        out_shape=tuple(pltpu.VMEM(w.shape, w.dtype) for w in weights) + (pltpu.VMEM((8, 128), jnp.float32),),
        in_specs=[pl.BlockSpec(memory_space=pltpu.HBM)] * 3 + [pl.BlockSpec(memory_space=pl.ANY)],
        out_specs=(in_vmem,) * 4,
        scratch_shapes=[pltpu.SemaphoreType.DMA((6,))],
        compiler_params=pltpu.CompilerParams(vmem_limit_bytes=12 << 20),
    )(*(in_hbm(w) for w in weights), rows)


def feed_kernel(*refs):
    blocks, (gate_ref, up_ref, down_ref, keep_ref, send_ref, far_ref, rows_ref) = refs[:-7], refs[-7:]
    at = 0
    for block in blocks:
        size = block.shape[0]
        rows_ref[pl.ds(at, size), :] = block[...]
        at += size
    rows = rows_ref[...]
    numbers = (((1,), (1,)), ((), ()))
    gate = lax.dot_general(gate_ref[...], rows, numbers, preferred_element_type=jnp.float32)
    up = lax.dot_general(up_ref[...], rows, numbers, preferred_element_type=jnp.float32)
    act = (gate / (1.0 + jnp.exp(-gate)) * up).T.astype(jnp.bfloat16)
    half = at // 2
    part = 1024
    for k in range(rows_ref.shape[1] // part):
        columns = pl.ds(k * part, part)
        feed = jnp.dot(act, down_ref[:, columns], preferred_element_type=jnp.float32)
        keep_ref[:, columns] = feed[:half]
        send_ref[:, columns] = feed[half : half + 48].astype(jnp.bfloat16)
        far_ref[:, columns] = feed[half + 48 :].astype(jnp.bfloat16)


def feed_rows(blocks, weights):
    width = weights[0].shape[-1]
    in_vmem = pl.BlockSpec(memory_space=pltpu.VMEM)
    held = [pltpu.with_memory_space_constraint(w, pltpu.VMEM) for w in weights]
    return pl.pallas_call(
        feed_kernel,
        out_shape=(
            pltpu.VMEM((64, width), jnp.float32),
            pltpu.VMEM((48, width), jnp.bfloat16),
            pltpu.VMEM((16, width), jnp.bfloat16),
        ),
        in_specs=[in_vmem] * (len(blocks) + 3),
        out_specs=(in_vmem,) * 3,
        scratch_shapes=[pltpu.VMEM((128, width), jnp.bfloat16)],
        compiler_params=pltpu.CompilerParams(vmem_limit_bytes=12 << 20),
    )(*blocks, *held)


def attend_kernel(
    length_ref,
    key_hbm,
    value_hbm,
    query_hbm,
    fresh_key_hbm,
    fresh_value_hbm,
    residual_hbm,
    gain_hbm,
    hidden_ref,
    normed_ref,
    keys,
    values,
    query,
    fresh_key,
    fresh_value,
    residual,
    gain,
    query_rows,
    residual_rows,
    sems,
):
    sources = (query_hbm, key_hbm, fresh_key_hbm, value_hbm, fresh_value_hbm, residual_hbm, gain_hbm)
    targets = (query, keys, fresh_key, values, fresh_value, residual, gain)
    copies = [pltpu.make_async_copy(s, t, sems.at[i]) for i, (s, t) in enumerate(zip(sources, targets))]
    for copy in copies:
        copy.start()
    copies[0].wait()
    for h in range(HEADS):
        query_rows[pl.ds(h, 1), :] = query[:, pl.ds(h * HD, HD)].astype(jnp.float32)
    slots = keys.shape[0]
    share = HEADS // KVH
    scale = HD ** (-0.5)
    usable = lax.broadcasted_iota(jnp.int32, (share, slots), 1) < length_ref[0, 0]
    copies[1].wait()
    copies[2].wait()
    weights = []
    for j in range(KVH):
        wide_query = query_rows[pl.ds(j * share, share), :]
        lanes = pl.ds(j * HD, HD)
        scores = lax.dot_general(
            wide_query.astype(jnp.bfloat16),
            keys[:, lanes],
            (((1,), (1,)), ((), ())),
            preferred_element_type=jnp.float32,
        )
        scores = jnp.where(usable, scores * scale, masked_score)
        fresh = jnp.sum(wide_query * fresh_key[:, lanes].astype(jnp.float32), axis=-1, keepdims=True) * scale
        ceiling = jnp.maximum(jnp.max(scores, axis=-1, keepdims=True), fresh)
        expo = jnp.where(usable, jnp.exp(scores - ceiling), 0.0)
        fresh_expo = jnp.exp(fresh - ceiling)
        denominator = jnp.sum(expo, axis=-1, keepdims=True) + fresh_expo
        weights.append((expo.astype(jnp.bfloat16), fresh_expo.astype(jnp.bfloat16), denominator))
    for copy in copies[3:]:
        copy.wait()
    for h in range(HEADS):
        residual_rows[pl.ds(h, 1), :] = residual[:, pl.ds(h * HD, HD)].astype(jnp.float32)
    square = jnp.zeros((1, 1), jnp.float32)
    for j in range(KVH):
        lanes = pl.ds(j * HD, HD)
        rows = pl.ds(j * share, share)
        expo, fresh_expo, denominator = weights[j]
        weighted = jnp.dot(expo, values[:, lanes], preferred_element_type=jnp.float32)
        weighted = weighted + fresh_expo.astype(jnp.float32) * fresh_value[:, lanes].astype(jnp.float32)
        hidden = residual_rows[rows, :] + weighted / denominator
        residual_rows[rows, :] = hidden
        square = square + jnp.sum(jnp.sum(hidden * hidden, axis=-1, keepdims=True), axis=0, keepdims=True)
    factor = lax.rsqrt(square / (HEADS * HD) + 1e-05)
    query_rows[...] = residual_rows[...] * factor * gain[...]
    for h in range(HEADS):
        lanes = pl.ds(h * HD, HD)
        hidden_ref[:, lanes] = residual_rows[pl.ds(h, 1), :]
        normed_ref[:, lanes] = query_rows[pl.ds(h, 1), :].astype(jnp.bfloat16)


def attend(lengths, key_cache, value_cache, queries, new_keys, new_values, residual, norm_gain):
    slots, columns = key_cache.shape[2:]
    width = queries.shape[-1]
    cache = (slots, columns)
    args = (
        lengths,
        key_cache.reshape(cache),
        value_cache.reshape(cache),
        queries.reshape(1, width),
        new_keys.reshape(1, columns),
        new_values.reshape(1, columns),
        residual.reshape(1, width),
        norm_gain.reshape(HEADS, HD),
    )
    in_vmem = pl.BlockSpec(memory_space=pltpu.VMEM)
    rows = pltpu.VMEM((HEADS, HD), jnp.float32)
    return pl.pallas_call(
        attend_kernel,
        out_shape=(
            jax.ShapeDtypeStruct((1, width), jnp.float32),
            jax.ShapeDtypeStruct((1, width), jnp.bfloat16),
        ),
        in_specs=[pl.BlockSpec(memory_space=pltpu.SMEM)] + [pl.BlockSpec(memory_space=pltpu.HBM)] * 7,
        out_specs=(in_vmem, in_vmem),
        scratch_shapes=[
            pltpu.VMEM(cache, jnp.bfloat16),
            pltpu.VMEM(cache, jnp.bfloat16),
            pltpu.VMEM((1, width), jnp.bfloat16),
            pltpu.VMEM((1, columns), jnp.bfloat16),
            pltpu.VMEM((1, columns), jnp.bfloat16),
            pltpu.VMEM((1, width), jnp.bfloat16),
            rows,
            rows,
            rows,
            pltpu.SemaphoreType.DMA((7,)),
        ],
        compiler_params=pltpu.CompilerParams(vmem_limit_bytes=16 << 20),
    )(args[0], *(in_hbm(arg) for arg in args[1:]))


def local(
    key_cache,
    value_cache,
    lengths,
    queries,
    new_keys,
    new_values,
    residual,
    norm_gain,
    gate_weight,
    up_weight,
    down_weight,
):
    serving = lax.axis_index("y") < lax.axis_size("y") // 2
    hidden, flat_rows = attend(
        lengths, key_cache, value_cache, queries, new_keys, new_values, residual, norm_gain
    )
    weights = gate_weight[0], up_weight[0], down_weight[0]
    summed = returned_rows(*feed_rows(*gathered_blocks(flat_rows, weights)))
    mixed = (hidden + summed).astype(jnp.bfloat16)
    mixed = jnp.where(serving, mixed, jnp.zeros_like(mixed))
    return mixed.reshape(residual.shape)


def solution(mesh):
    finer = Mesh(mesh.devices.reshape(4, 2, 8, 2, 2), ("y", "xh", "z", "xl", "c"))
    in_specs = (
        P(GRP, TP, None, None),
        P(GRP, TP, None, None),
        P(GRP, TP),
        P(GRP, None, TP, None),
        P(GRP, None, TP, None),
        P(GRP, None, TP, None),
        P(GRP, None, TP, None),
        P(),
        P(GRP, TP, None),
        P(GRP, TP, None),
        P(GRP, TP, None),
    )
    out_specs = P(GRP, None, TP, None)
    return jax.shard_map(local, mesh=finer, in_specs=in_specs, out_specs=out_specs, check_vma=False)
```

```python
import jax
import jax.numpy as jnp
from jax import lax
from jax.experimental import pallas as pl
from jax.experimental.pallas import tpu as pltpu
from jax.sharding import Mesh
from jax.sharding import PartitionSpec as P

HEADS = 64
HD = 128
KVH = 4
X = ("xh", "xl")
GRP = ("y", "xh")
TP = ("z", "xl", "c")


masked_score = -1e30


def shifted(value, axes, hops):
    size = lax.axis_size(axes)
    return lax.ppermute(value, axes, [(i, (i + hops) % size) for i in range(size)])


def swapped(value):
    return shifted(value, "c", 1)


def mirrored(value):
    return lax.ppermute(value, "y", [(i, 3 - i) for i in range(4)])


def opposite(value):
    return lax.ppermute(value, "y", [(i, (i + 2) % 4) for i in range(4)])


def in_hbm(value):
    return pltpu.with_memory_space_constraint(value, pltpu.HBM)


def wide(value):
    return value.astype(jnp.float32)


def narrow(value):
    return value.astype(jnp.bfloat16)


def spread_kernel(near_ref, far_ref, copies_ref):
    near, far = near_ref[...], far_ref[...]
    for i in range(copies_ref.shape[0]):
        copies_ref[i, pl.ds(0, 1), :] = near
        copies_ref[i, pl.ds(1, 1), :] = far


def spread(near, far):
    in_vmem = pl.BlockSpec(memory_space=pltpu.VMEM)
    return pl.pallas_call(
        spread_kernel,
        out_shape=pltpu.VMEM((8, 2, near.shape[-1]), near.dtype),
        in_specs=[in_vmem, in_vmem],
        out_specs=in_vmem,
        compiler_params=pltpu.CompilerParams(vmem_limit_bytes=4 << 20),
    )(near, far)


def pairs_kernel(pairs_ref, rows_ref):
    for i in range(pairs_ref.shape[0]):
        rows_ref[pl.ds(2 * i, 2), :] = pairs_ref[i]


def rows_of_pairs(pairs):
    count, _, width = pairs.shape
    in_vmem = pl.BlockSpec(memory_space=pltpu.VMEM)
    return pl.pallas_call(
        pairs_kernel,
        out_shape=pltpu.VMEM((2 * count, width), pairs.dtype),
        in_specs=[in_vmem],
        out_specs=in_vmem,
        compiler_params=pltpu.CompilerParams(vmem_limit_bytes=4 << 20),
    )(pairs)


def onward_kernel(rows_ref, token_ref, copy_ref):
    copy_ref[...] = rows_ref[...]


def onward(rows, token):
    in_vmem = pl.BlockSpec(memory_space=pltpu.VMEM)
    return pl.pallas_call(
        onward_kernel,
        out_shape=pltpu.VMEM(rows.shape, rows.dtype),
        in_specs=[in_vmem, pl.BlockSpec(memory_space=pl.ANY)],
        out_specs=in_vmem,
        compiler_params=pltpu.CompilerParams(vmem_limit_bytes=4 << 20),
    )(rows, token)


def along_x(value, hops):
    pairs = [(x * 2 + c, (x + (1 - 2 * c) * hops) % 4 * 2 + c) for x in range(4) for c in range(2)]
    return lax.ppermute(value, X + ("c",), pairs)


def gathered_blocks(row, weights):
    copies = spread(mirrored(row), opposite(row))
    pairs = lax.all_to_all(copies, "z", 0, 0, tiled=True)
    block = rows_of_pairs(pairs)
    *weights, token = loaded(weights, block)
    near = along_x(block, 1)
    far = along_x(near, 1)
    back = along_x(onward(block, token), -1)
    kept = [block, near, swapped(back), far]
    return kept + [swapped(block), swapped(near), back, swapped(far)], weights


def returned_rows(keep, send, send_far):
    far = keep[48:] + wide(swapped(send_far))
    rest = keep[:48] + wide(swapped(send))
    own, near, near_other = rest[:16], rest[16:32], rest[32:]
    far_in = along_x(narrow(far), -1)
    other_in = along_x(narrow(near_other), -1)
    near_in = along_x(narrow(near + wide(far_in)), -1)
    own = narrow(own + wide(swapped(other_in)) + wide(near_in))
    depth = lax.axis_size("z")
    pieces = own.reshape(depth, 2, own.shape[-1])
    arrived = lax.all_to_all(pieces, "z", 0, 0, tiled=True)
    pair = jnp.sum(arrived.astype(jnp.float32), axis=0)
    return mirrored(pair[:1]) + opposite(pair[1:])


def load_kernel(*refs):
    sources, targets, token_ref, sems = refs[:3], refs[4:7], refs[7], refs[8]
    copies = []
    parts = 2
    for w, (source, target) in enumerate(zip(sources, targets)):
        size = source.shape[0] // parts
        for i in range(parts):
            rows = pl.ds(i * size, size)
            copies.append(pltpu.make_async_copy(source.at[rows], target.at[rows], sems.at[w * parts + i]))
    for copy in copies:
        copy.start()
    token_ref[...] = jnp.zeros_like(token_ref)
    for copy in copies:
        copy.wait()


def loaded(weights, rows):
    in_vmem = pl.BlockSpec(memory_space=pltpu.VMEM)
    return pl.pallas_call(
        load_kernel,
        out_shape=tuple(pltpu.VMEM(w.shape, w.dtype) for w in weights) + (pltpu.VMEM((8, 128), jnp.float32),),
        in_specs=[pl.BlockSpec(memory_space=pltpu.HBM)] * 3 + [pl.BlockSpec(memory_space=pl.ANY)],
        out_specs=(in_vmem,) * 4,
        scratch_shapes=[pltpu.SemaphoreType.DMA((6,))],
        compiler_params=pltpu.CompilerParams(vmem_limit_bytes=12 << 20),
    )(*(in_hbm(w) for w in weights), rows)


def feed_kernel(*refs):
    blocks, (gate_ref, up_ref, down_ref, keep_ref, send_ref, far_ref, rows_ref) = refs[:-7], refs[-7:]
    at = 0
    for block in blocks:
        size = block.shape[0]
        rows_ref[pl.ds(at, size), :] = block[...]
        at += size
    rows = rows_ref[...]
    numbers = (((1,), (1,)), ((), ()))
    gate = lax.dot_general(gate_ref[...], rows, numbers, preferred_element_type=jnp.float32)
    up = lax.dot_general(up_ref[...], rows, numbers, preferred_element_type=jnp.float32)
    act = (gate / (1.0 + jnp.exp(-gate)) * up).T.astype(jnp.bfloat16)
    half = at // 2
    part = 1024
    for k in range(rows_ref.shape[1] // part):
        columns = pl.ds(k * part, part)
        feed = jnp.dot(act, down_ref[:, columns], preferred_element_type=jnp.float32)
        keep_ref[:, columns] = feed[:half]
        send_ref[:, columns] = feed[half : half + 48].astype(jnp.bfloat16)
        far_ref[:, columns] = feed[half + 48 :].astype(jnp.bfloat16)


def feed_rows(blocks, weights):
    width = weights[0].shape[-1]
    in_vmem = pl.BlockSpec(memory_space=pltpu.VMEM)
    held = [pltpu.with_memory_space_constraint(w, pltpu.VMEM) for w in weights]
    return pl.pallas_call(
        feed_kernel,
        out_shape=(
            pltpu.VMEM((64, width), jnp.float32),
            pltpu.VMEM((48, width), jnp.bfloat16),
            pltpu.VMEM((16, width), jnp.bfloat16),
        ),
        in_specs=[in_vmem] * (len(blocks) + 3),
        out_specs=(in_vmem,) * 3,
        scratch_shapes=[pltpu.VMEM((128, width), jnp.bfloat16)],
        compiler_params=pltpu.CompilerParams(vmem_limit_bytes=12 << 20),
    )(*blocks, *held)


def attend_kernel(
    length_ref,
    key_hbm,
    value_hbm,
    query_hbm,
    fresh_key_hbm,
    fresh_value_hbm,
    residual_hbm,
    gain_hbm,
    hidden_ref,
    normed_ref,
    keys,
    values,
    query,
    fresh_key,
    fresh_value,
    residual,
    gain,
    query_rows,
    residual_rows,
    sems,
):
    sources = (query_hbm, key_hbm, fresh_key_hbm, value_hbm, fresh_value_hbm, residual_hbm, gain_hbm)
    targets = (query, keys, fresh_key, values, fresh_value, residual, gain)
    copies = [pltpu.make_async_copy(s, t, sems.at[i]) for i, (s, t) in enumerate(zip(sources, targets))]
    for copy in copies:
        copy.start()
    copies[0].wait()
    for h in range(HEADS):
        query_rows[pl.ds(h, 1), :] = query[:, pl.ds(h * HD, HD)].astype(jnp.float32)
    slots = keys.shape[0]
    share = HEADS // KVH
    scale = HD ** (-0.5)
    usable = lax.broadcasted_iota(jnp.int32, (share, slots), 1) < length_ref[0, 0]
    copies[1].wait()
    copies[2].wait()
    weights = []
    for j in range(KVH):
        wide_query = query_rows[pl.ds(j * share, share), :]
        lanes = pl.ds(j * HD, HD)
        scores = lax.dot_general(
            wide_query.astype(jnp.bfloat16),
            keys[:, lanes],
            (((1,), (1,)), ((), ())),
            preferred_element_type=jnp.float32,
        )
        scores = jnp.where(usable, scores * scale, masked_score)
        fresh = jnp.sum(wide_query * fresh_key[:, lanes].astype(jnp.float32), axis=-1, keepdims=True) * scale
        ceiling = jnp.maximum(jnp.max(scores, axis=-1, keepdims=True), fresh)
        expo = jnp.where(usable, jnp.exp(scores - ceiling), 0.0)
        fresh_expo = jnp.exp(fresh - ceiling)
        denominator = jnp.sum(expo, axis=-1, keepdims=True) + fresh_expo
        weights.append((expo.astype(jnp.bfloat16), fresh_expo.astype(jnp.bfloat16), denominator))
    for copy in copies[3:]:
        copy.wait()
    for h in range(HEADS):
        residual_rows[pl.ds(h, 1), :] = residual[:, pl.ds(h * HD, HD)].astype(jnp.float32)
    square = jnp.zeros((1, 1), jnp.float32)
    for j in range(KVH):
        lanes = pl.ds(j * HD, HD)
        rows = pl.ds(j * share, share)
        expo, fresh_expo, denominator = weights[j]
        weighted = jnp.dot(expo, values[:, lanes], preferred_element_type=jnp.float32)
        weighted = weighted + fresh_expo.astype(jnp.float32) * fresh_value[:, lanes].astype(jnp.float32)
        hidden = residual_rows[rows, :] + weighted / denominator
        residual_rows[rows, :] = hidden
        square = square + jnp.sum(jnp.sum(hidden * hidden, axis=-1, keepdims=True), axis=0, keepdims=True)
    factor = lax.rsqrt(square / (HEADS * HD) + 1e-05)
    query_rows[...] = residual_rows[...] * factor * gain[...]
    for h in range(HEADS):
        lanes = pl.ds(h * HD, HD)
        hidden_ref[:, lanes] = residual_rows[pl.ds(h, 1), :]
        normed_ref[:, lanes] = query_rows[pl.ds(h, 1), :].astype(jnp.bfloat16)


def attend(lengths, key_cache, value_cache, queries, new_keys, new_values, residual, norm_gain):
    slots, columns = key_cache.shape[2:]
    width = queries.shape[-1]
    cache = (slots, columns)
    args = (
        lengths,
        key_cache.reshape(cache),
        value_cache.reshape(cache),
        queries.reshape(1, width),
        new_keys.reshape(1, columns),
        new_values.reshape(1, columns),
        residual.reshape(1, width),
        norm_gain.reshape(HEADS, HD),
    )
    in_vmem = pl.BlockSpec(memory_space=pltpu.VMEM)
    rows = pltpu.VMEM((HEADS, HD), jnp.float32)
    return pl.pallas_call(
        attend_kernel,
        out_shape=(
            jax.ShapeDtypeStruct((1, width), jnp.float32),
            jax.ShapeDtypeStruct((1, width), jnp.bfloat16),
        ),
        in_specs=[pl.BlockSpec(memory_space=pltpu.SMEM)] + [pl.BlockSpec(memory_space=pltpu.HBM)] * 7,
        out_specs=(in_vmem, in_vmem),
        scratch_shapes=[
            pltpu.VMEM(cache, jnp.bfloat16),
            pltpu.VMEM(cache, jnp.bfloat16),
            pltpu.VMEM((1, width), jnp.bfloat16),
            pltpu.VMEM((1, columns), jnp.bfloat16),
            pltpu.VMEM((1, columns), jnp.bfloat16),
            pltpu.VMEM((1, width), jnp.bfloat16),
            rows,
            rows,
            rows,
            pltpu.SemaphoreType.DMA((7,)),
        ],
        compiler_params=pltpu.CompilerParams(vmem_limit_bytes=16 << 20),
    )(args[0], *(in_hbm(arg) for arg in args[1:]))


def local(
    key_cache,
    value_cache,
    lengths,
    queries,
    new_keys,
    new_values,
    residual,
    norm_gain,
    gate_weight,
    up_weight,
    down_weight,
):
    serving = lax.axis_index("y") < lax.axis_size("y") // 2
    hidden, flat_rows = attend(
        lengths, key_cache, value_cache, queries, new_keys, new_values, residual, norm_gain
    )
    weights = gate_weight[0], up_weight[0], down_weight[0]
    summed = returned_rows(*feed_rows(*gathered_blocks(flat_rows, weights)))
    mixed = (hidden + summed).astype(jnp.bfloat16)
    mixed = jnp.where(serving, mixed, jnp.zeros_like(mixed))
    return mixed.reshape(residual.shape)


def solution(mesh):
    finer = Mesh(mesh.devices.reshape(4, 2, 8, 2, 2), ("y", "xh", "z", "xl", "c"))
    in_specs = (
        P(GRP, TP, None, None),
        P(GRP, TP, None, None),
        P(GRP, TP),
        P(GRP, None, TP, None),
        P(GRP, None, TP, None),
        P(GRP, None, TP, None),
        P(GRP, None, TP, None),
        P(),
        P(GRP, TP, None),
        P(GRP, TP, None),
        P(GRP, TP, None),
    )
    out_specs = P(GRP, None, TP, None)
    return jax.shard_map(local, mesh=finer, in_specs=in_specs, out_specs=out_specs, check_vma=False)
```

```python
import jax
import jax.numpy as jnp
from jax import lax
from jax.experimental import pallas as pl
from jax.experimental.pallas import tpu as pltpu
from jax.sharding import Mesh
from jax.sharding import PartitionSpec as P

HEADS = 64
HD = 128
KVH = 4
X = ("xh", "xl")
GRP = ("y", "xh")
TP = ("z", "xl", "c")


masked_score = -1e30


def shifted(value, axes, hops):
    size = lax.axis_size(axes)
    return lax.ppermute(value, axes, [(i, (i + hops) % size) for i in range(size)])


def swapped(value):
    return shifted(value, "c", 1)


def mirrored(value):
    return lax.ppermute(value, "y", [(i, 3 - i) for i in range(4)])


def opposite(value):
    return lax.ppermute(value, "y", [(i, (i + 2) % 4) for i in range(4)])


def in_hbm(value):
    return pltpu.with_memory_space_constraint(value, pltpu.HBM)


def wide(value):
    return value.astype(jnp.float32)


def narrow(value):
    return value.astype(jnp.bfloat16)


def spread_kernel(near_ref, far_ref, copies_ref):
    near, far = near_ref[...], far_ref[...]
    for i in range(copies_ref.shape[0]):
        copies_ref[i, pl.ds(0, 1), :] = near
        copies_ref[i, pl.ds(1, 1), :] = far


def spread(near, far):
    in_vmem = pl.BlockSpec(memory_space=pltpu.VMEM)
    return pl.pallas_call(
        spread_kernel,
        out_shape=pltpu.VMEM((8, 2, near.shape[-1]), near.dtype),
        in_specs=[in_vmem, in_vmem],
        out_specs=in_vmem,
        compiler_params=pltpu.CompilerParams(vmem_limit_bytes=4 << 20),
    )(near, far)


def pairs_kernel(pairs_ref, rows_ref):
    for i in range(pairs_ref.shape[0]):
        rows_ref[pl.ds(2 * i, 2), :] = pairs_ref[i]


def rows_of_pairs(pairs):
    count, _, width = pairs.shape
    in_vmem = pl.BlockSpec(memory_space=pltpu.VMEM)
    return pl.pallas_call(
        pairs_kernel,
        out_shape=pltpu.VMEM((2 * count, width), pairs.dtype),
        in_specs=[in_vmem],
        out_specs=in_vmem,
        compiler_params=pltpu.CompilerParams(vmem_limit_bytes=4 << 20),
    )(pairs)


def onward_kernel(rows_ref, token_ref, copy_ref):
    copy_ref[...] = rows_ref[...]


def onward(rows, token):
    in_vmem = pl.BlockSpec(memory_space=pltpu.VMEM)
    return pl.pallas_call(
        onward_kernel,
        out_shape=pltpu.VMEM(rows.shape, rows.dtype),
        in_specs=[in_vmem, pl.BlockSpec(memory_space=pl.ANY)],
        out_specs=in_vmem,
        compiler_params=pltpu.CompilerParams(vmem_limit_bytes=4 << 20),
    )(rows, token)


def along_x(value, hops):
    pairs = [(x * 2 + c, (x + (1 - 2 * c) * hops) % 4 * 2 + c) for x in range(4) for c in range(2)]
    return lax.ppermute(value, X + ("c",), pairs)


def gathered_blocks(row, weights):
    copies = spread(mirrored(row), opposite(row))
    pairs = lax.all_to_all(copies, "z", 0, 0, tiled=True)
    block = rows_of_pairs(pairs)
    *weights, token = loaded(weights, block)
    near = along_x(block, 1)
    far = along_x(near, 1)
    back = along_x(onward(block, token), -1)
    kept = [block, near, swapped(back), far]
    return kept + [swapped(block), swapped(near), back, swapped(far)], weights


def returned_rows(keep, send, send_far):
    far = keep[48:] + wide(swapped(send_far))
    rest = keep[:48] + wide(swapped(send))
    own, near, near_other = rest[:16], rest[16:32], rest[32:]
    far_in = along_x(narrow(far), -1)
    other_in = along_x(narrow(near_other), -1)
    near_in = along_x(narrow(near + wide(far_in)), -1)
    own = narrow(own + wide(swapped(other_in)) + wide(near_in))
    depth = lax.axis_size("z")
    pieces = own.reshape(depth, 2, own.shape[-1])
    arrived = lax.all_to_all(pieces, "z", 0, 0, tiled=True)
    pair = jnp.sum(arrived.astype(jnp.float32), axis=0)
    return mirrored(pair[:1]) + opposite(pair[1:])


def load_kernel(*refs):
    sources, targets, token_ref, sems = refs[:3], refs[4:7], refs[7], refs[8]
    copies = []
    parts = 13
    for w, (source, target) in enumerate(zip(sources, targets)):
        size = source.shape[0] // parts
        for i in range(parts):
            rows = pl.ds(i * size, size)
            copies.append(pltpu.make_async_copy(source.at[rows], target.at[rows], sems.at[w * parts + i]))
    for copy in copies:
        copy.start()
    token_ref[...] = jnp.zeros_like(token_ref)
    for copy in copies:
        copy.wait()


def loaded(weights, rows):
    in_vmem = pl.BlockSpec(memory_space=pltpu.VMEM)
    return pl.pallas_call(
        load_kernel,
        out_shape=tuple(pltpu.VMEM(w.shape, w.dtype) for w in weights) + (pltpu.VMEM((8, 128), jnp.float32),),
        in_specs=[pl.BlockSpec(memory_space=pltpu.HBM)] * 3 + [pl.BlockSpec(memory_space=pl.ANY)],
        out_specs=(in_vmem,) * 4,
        scratch_shapes=[pltpu.SemaphoreType.DMA((39,))],
        compiler_params=pltpu.CompilerParams(vmem_limit_bytes=12 << 20),
    )(*(in_hbm(w) for w in weights), rows)


def feed_kernel(*refs):
    blocks, (gate_ref, up_ref, down_ref, keep_ref, send_ref, far_ref, rows_ref) = refs[:-7], refs[-7:]
    at = 0
    for block in blocks:
        size = block.shape[0]
        rows_ref[pl.ds(at, size), :] = block[...]
        at += size
    rows = rows_ref[...]
    numbers = (((1,), (1,)), ((), ()))
    gate = lax.dot_general(gate_ref[...], rows, numbers, preferred_element_type=jnp.float32)
    up = lax.dot_general(up_ref[...], rows, numbers, preferred_element_type=jnp.float32)
    act = (gate / (1.0 + jnp.exp(-gate)) * up).T.astype(jnp.bfloat16)
    half = at // 2
    part = 1024
    for k in range(rows_ref.shape[1] // part):
        columns = pl.ds(k * part, part)
        feed = jnp.dot(act, down_ref[:, columns], preferred_element_type=jnp.float32)
        keep_ref[:, columns] = feed[:half]
        send_ref[:, columns] = feed[half : half + 48].astype(jnp.bfloat16)
        far_ref[:, columns] = feed[half + 48 :].astype(jnp.bfloat16)


def feed_rows(blocks, weights):
    width = weights[0].shape[-1]
    in_vmem = pl.BlockSpec(memory_space=pltpu.VMEM)
    held = [pltpu.with_memory_space_constraint(w, pltpu.VMEM) for w in weights]
    return pl.pallas_call(
        feed_kernel,
        out_shape=(
            pltpu.VMEM((64, width), jnp.float32),
            pltpu.VMEM((48, width), jnp.bfloat16),
            pltpu.VMEM((16, width), jnp.bfloat16),
        ),
        in_specs=[in_vmem] * (len(blocks) + 3),
        out_specs=(in_vmem,) * 3,
        scratch_shapes=[pltpu.VMEM((128, width), jnp.bfloat16)],
        compiler_params=pltpu.CompilerParams(vmem_limit_bytes=12 << 20),
    )(*blocks, *held)


def attend_kernel(
    length_ref,
    key_hbm,
    value_hbm,
    query_hbm,
    fresh_key_hbm,
    fresh_value_hbm,
    residual_hbm,
    gain_hbm,
    hidden_ref,
    normed_ref,
    keys,
    values,
    query,
    fresh_key,
    fresh_value,
    residual,
    gain,
    query_rows,
    residual_rows,
    sems,
):
    sources = (query_hbm, key_hbm, fresh_key_hbm, value_hbm, fresh_value_hbm, residual_hbm, gain_hbm)
    targets = (query, keys, fresh_key, values, fresh_value, residual, gain)
    copies = [pltpu.make_async_copy(s, t, sems.at[i]) for i, (s, t) in enumerate(zip(sources, targets))]
    for copy in copies:
        copy.start()
    copies[0].wait()
    for h in range(HEADS):
        query_rows[pl.ds(h, 1), :] = query[:, pl.ds(h * HD, HD)].astype(jnp.float32)
    slots = keys.shape[0]
    share = HEADS // KVH
    scale = HD ** (-0.5)
    usable = lax.broadcasted_iota(jnp.int32, (share, slots), 1) < length_ref[0, 0]
    copies[1].wait()
    copies[2].wait()
    weights = []
    for j in range(KVH):
        wide_query = query_rows[pl.ds(j * share, share), :]
        lanes = pl.ds(j * HD, HD)
        scores = lax.dot_general(
            wide_query.astype(jnp.bfloat16),
            keys[:, lanes],
            (((1,), (1,)), ((), ())),
            preferred_element_type=jnp.float32,
        )
        scores = jnp.where(usable, scores * scale, masked_score)
        fresh = jnp.sum(wide_query * fresh_key[:, lanes].astype(jnp.float32), axis=-1, keepdims=True) * scale
        ceiling = jnp.maximum(jnp.max(scores, axis=-1, keepdims=True), fresh)
        expo = jnp.where(usable, jnp.exp(scores - ceiling), 0.0)
        fresh_expo = jnp.exp(fresh - ceiling)
        denominator = jnp.sum(expo, axis=-1, keepdims=True) + fresh_expo
        weights.append((expo.astype(jnp.bfloat16), fresh_expo.astype(jnp.bfloat16), denominator))
    for copy in copies[3:]:
        copy.wait()
    for h in range(HEADS):
        residual_rows[pl.ds(h, 1), :] = residual[:, pl.ds(h * HD, HD)].astype(jnp.float32)
    square = jnp.zeros((1, 1), jnp.float32)
    for j in range(KVH):
        lanes = pl.ds(j * HD, HD)
        rows = pl.ds(j * share, share)
        expo, fresh_expo, denominator = weights[j]
        weighted = jnp.dot(expo, values[:, lanes], preferred_element_type=jnp.float32)
        weighted = weighted + fresh_expo.astype(jnp.float32) * fresh_value[:, lanes].astype(jnp.float32)
        hidden = residual_rows[rows, :] + weighted / denominator
        residual_rows[rows, :] = hidden
        square = square + jnp.sum(jnp.sum(hidden * hidden, axis=-1, keepdims=True), axis=0, keepdims=True)
    factor = lax.rsqrt(square / (HEADS * HD) + 1e-05)
    query_rows[...] = residual_rows[...] * factor * gain[...]
    for h in range(HEADS):
        lanes = pl.ds(h * HD, HD)
        hidden_ref[:, lanes] = residual_rows[pl.ds(h, 1), :]
        normed_ref[:, lanes] = query_rows[pl.ds(h, 1), :].astype(jnp.bfloat16)


def attend(lengths, key_cache, value_cache, queries, new_keys, new_values, residual, norm_gain):
    slots, columns = key_cache.shape[2:]
    width = queries.shape[-1]
    cache = (slots, columns)
    args = (
        lengths,
        key_cache.reshape(cache),
        value_cache.reshape(cache),
        queries.reshape(1, width),
        new_keys.reshape(1, columns),
        new_values.reshape(1, columns),
        residual.reshape(1, width),
        norm_gain.reshape(HEADS, HD),
    )
    in_vmem = pl.BlockSpec(memory_space=pltpu.VMEM)
    rows = pltpu.VMEM((HEADS, HD), jnp.float32)
    return pl.pallas_call(
        attend_kernel,
        out_shape=(
            jax.ShapeDtypeStruct((1, width), jnp.float32),
            jax.ShapeDtypeStruct((1, width), jnp.bfloat16),
        ),
        in_specs=[pl.BlockSpec(memory_space=pltpu.SMEM)] + [pl.BlockSpec(memory_space=pltpu.HBM)] * 7,
        out_specs=(in_vmem, in_vmem),
        scratch_shapes=[
            pltpu.VMEM(cache, jnp.bfloat16),
            pltpu.VMEM(cache, jnp.bfloat16),
            pltpu.VMEM((1, width), jnp.bfloat16),
            pltpu.VMEM((1, columns), jnp.bfloat16),
            pltpu.VMEM((1, columns), jnp.bfloat16),
            pltpu.VMEM((1, width), jnp.bfloat16),
            rows,
            rows,
            rows,
            pltpu.SemaphoreType.DMA((7,)),
        ],
        compiler_params=pltpu.CompilerParams(vmem_limit_bytes=16 << 20),
    )(args[0], *(in_hbm(arg) for arg in args[1:]))


def local(
    key_cache,
    value_cache,
    lengths,
    queries,
    new_keys,
    new_values,
    residual,
    norm_gain,
    gate_weight,
    up_weight,
    down_weight,
):
    serving = lax.axis_index("y") < lax.axis_size("y") // 2
    hidden, flat_rows = attend(
        lengths, key_cache, value_cache, queries, new_keys, new_values, residual, norm_gain
    )
    weights = gate_weight[0], up_weight[0], down_weight[0]
    summed = returned_rows(*feed_rows(*gathered_blocks(flat_rows, weights)))
    mixed = (hidden + summed).astype(jnp.bfloat16)
    mixed = jnp.where(serving, mixed, jnp.zeros_like(mixed))
    return mixed.reshape(residual.shape)


def solution(mesh):
    finer = Mesh(mesh.devices.reshape(4, 2, 8, 2, 2), ("y", "xh", "z", "xl", "c"))
    in_specs = (
        P(GRP, TP, None, None),
        P(GRP, TP, None, None),
        P(GRP, TP),
        P(GRP, None, TP, None),
        P(GRP, None, TP, None),
        P(GRP, None, TP, None),
        P(GRP, None, TP, None),
        P(),
        P(GRP, TP, None),
        P(GRP, TP, None),
        P(GRP, TP, None),
    )
    out_specs = P(GRP, None, TP, None)
    return jax.shard_map(local, mesh=finer, in_specs=in_specs, out_specs=out_specs, check_vma=False)
```
